32 devices in a mesh: grp: 2 (over y), tm: 4 (over z), tmpl: 2 (over x), chan: 2 (over core).
Axes of the slice: x: 2, y: 2, z: 4, core: 2. Of those that a mesh axis runs over, the one named last changes fastest.
Arguments:
- record: bfloat16 [32, 4096], P('chan', ('grp', 'tm')), parts along dimension 1, may hold values from -640 to 640
- templates: bfloat16 [2, 768, 32, 512], P('tmpl', 'tm', 'chan'), may hold values from -0.046875 to 0.046875
- span_list: int32 [8, 4], P(('grp', 'tm')), parts along dimension 0, may hold values from -1 to 3, as said below
Outputs:
- scan_out: float32 [1536, 4096], P(('tmpl', 'chan'), ('grp', 'tm')), parts along dimension 1
The draws below stay inside these ranges and needn't reach their ends.
There are 2 independent parts, one for each index of `grp`. The reference program is written for one: setup_inputs(seed, part) draws one part's arguments, and reference() takes and returns one part's arrays. A program takes and returns all parts, laid end to end along the dimension named above; an argument that names none is the same for every part. Nothing has to cross between parts.
Inputs may be any that keep to these rules, and one draw needn't show every extreme that they name: `span_list`: each shard lists distinct blocks in its first slots and -1 in the rest; between 1 and 4 blocks a shard, exactly 8 in all shards together, and some shard lists 4.
All inputs are finite; a program needn't handle non-finite values.
Results may differ from the reference program's by a relative error of at most 0.0003.
Values may be sent and summed in bfloat16 or wider, within the bound.
A program may use at most 64 MiB of HBM per device.

```python
import math
import jax
import jax.numpy as jnp
import numpy as np
from jax import lax

C = 32
L = 512
K = 1536
SPAN = 128
NCH_DEV = 4
MOST_DENSE = 4
TIME = 2048
KG = 768
DENSE_TOTAL = 8
N_TM = 4
N_TMPL = 2


def draw_record(key, part):
    keys = jax.random.split(jax.random.fold_in(key, 11), 3)
    blocks = TIME // 8
    spread = math.log(10.0)
    base = jax.random.truncated_normal(keys[0], -4.0, 4.0, (C, TIME), jnp.float32)
    chan_scale = jnp.exp(jax.random.uniform(keys[1], (C, 1), jnp.float32, 0.0, spread))
    time_scale = jnp.exp(jax.random.uniform(keys[2], (1, blocks), jnp.float32, 0.0, spread))
    time_scale = jnp.repeat(time_scale, 8, axis=1)
    return (base * chan_scale * time_scale).astype(jnp.bfloat16)


def draw_span_list(key, part):
    keys = jax.random.split(jax.random.fold_in(key, 23), N_TM + 1)
    pattern = np.zeros(N_TM, np.int32)
    pattern[0] = 2
    pattern[1] = -1
    pattern[2] = -1
    for place in range(3, N_TM):
        if place % 2 == 1 and place + 1 < N_TM:
            pattern[place] = 1
        elif place % 2 == 0:
            pattern[place] = -1
    order = jax.random.permutation(keys[0], N_TM)
    counts = jnp.zeros((N_TM,), jnp.int32).at[order].set(jnp.asarray(pattern + 2, jnp.int32))
    picks = jax.vmap(lambda sub: jax.random.permutation(sub, NCH_DEV)[:MOST_DENSE])(keys[1:])
    column = jnp.arange(MOST_DENSE, dtype=jnp.int32)[None, :]
    return jnp.where(column < counts[:, None], picks.astype(jnp.int32), -1).astype(jnp.int32)


def block_scale(rng, extent, shards, low, largest):
    level = 1.0
    for position, blocks in shards:
        heights = jax.random.uniform(jax.random.fold_in(jax.random.fold_in(rng, 6), position), (blocks,), jnp.float32, low / len(shards), largest / len(shards))
        level = level * jnp.repeat(jnp.exp(heights), extent[position] // blocks).reshape((-1,) + (1,) * (len(extent) - 1 - position))
    return level


def scatter_about(key, dims, scale, bound, pieces=(), kind=jnp.bfloat16):
    drawn = scale * jax.random.normal(key, dims, jnp.float32)
    if pieces:
        drawn = drawn * block_scale(key, dims, pieces, -0.22, 0.18)
    return jnp.clip(drawn, -bound, bound).astype(kind)


def setup_inputs(seed: int = 0, part: int = 0) -> dict:
    key_of = jax.random.split(jax.random.key(seed), 4)
    part_splits = jax.random.split(jax.random.fold_in(key_of[3], part), 4)
    return {
        "record": draw_record(jax.random.fold_in(jax.random.fold_in(key_of[3], part), 71), part),
        "templates": scatter_about(key_of[1], (N_TMPL, KG, C, L), (C * L) ** -0.5, 0.046875, ((0, 2), (1, 4), (2, 2))),
        "span_list": draw_span_list(jax.random.fold_in(jax.random.fold_in(key_of[3], part), 71), part),
    }


def windows(segment):
    seg_len = segment.shape[1]
    tiled = jnp.tile(segment, (1, SPAN + 1))
    flattened = tiled[:, :SPAN * (seg_len + 1)]
    return flattened.reshape(segment.shape[0], SPAN, seg_len + 1)[:, :, :L]

def reference(record, templates, span_list):
    shard_len = NCH_DEV * SPAN
    padded = jnp.concatenate([record, jnp.zeros((C, shard_len), record.dtype)], axis=1)
    flat_tmpl = templates.reshape(K, C * L)
    listed = span_list.reshape(-1).astype(jnp.int32)
    usable = (listed >= 0).astype(jnp.int32)
    chosen = jnp.argsort(1 - usable, stable=True)[:DENSE_TOTAL].astype(jnp.int32)

    def one_slot(slot_index):
        span_at = listed[slot_index]
        sample_start = (slot_index // MOST_DENSE * shard_len + span_at * SPAN).astype(jnp.int32)
        segment = lax.dynamic_slice_in_dim(padded, sample_start, SPAN + L, 1)
        window_set = windows(segment)
        columns = window_set.transpose(0, 2, 1).reshape(C * L, SPAN)
        correlation = jnp.dot(flat_tmpl, columns, preferred_element_type=jnp.float32)
        energy = lax.optimization_barrier(jnp.sum(jnp.square(window_set.astype(jnp.float32)), axis=(0, 2)))
        return correlation * lax.rsqrt(energy / (C * L) + 1e-05)[None, :]
    results = lax.map(one_slot, chosen)
    scattered = jnp.zeros((N_TM * MOST_DENSE, K, SPAN), jnp.float32).at[chosen].set(results)
    return scattered.transpose(1, 0, 2).reshape(K, N_TM * MOST_DENSE * SPAN)
```

```python
import functools

import jax
import jax.numpy as jnp
from jax import lax
from jax.experimental import pallas as pl
from jax.experimental.pallas import tpu as pltpu
from jax.sharding import PartitionSpec as P

SPAN = 128
CODES = 32767.0
MESH = pl.DeviceIdType.MESH


def kernel(n, rows, chans, slots, span_ref, rec_ref, tmpl_ref, out_ref, tmpl, lhs, rec_all, ring_a, ring_b, ring_c, ring_d, acc, sib, codes, scales,
           codes_in, scales_in, e_mine, e_sib, rec_send, rec_recv, sib_send, sib_recv, code_send, code_recv,
           scale_send, scale_recv, e_send, e_recv, tmpl_sem):
    z = lax.axis_index("tm")
    core = lax.axis_index("chan")
    half = n // 2
    home = z // half
    own_part = z % half
    other = {"tm": z, "chan": 1 - core}
    ring = (ring_a, ring_b, ring_c, ring_d)

    tmpl_copy = pltpu.make_async_copy(tmpl_ref.at[0], tmpl, tmpl_sem)
    tmpl_copy.start()
    barrier = pltpu.get_barrier_semaphore()

    def greet(i, _):
        peer = lax.rem(z + i // 2, n)
        to = lax.rem(core + i % 2, 2)
        pl.semaphore_signal(barrier, inc=1, device_id={"tm": peer, "chan": to}, device_id_type=MESH)
        return 0

    lax.fori_loop(1, 2 * n, greet, 0)
    rec_all[z] = rec_ref[...]
    rec_all[n] = jnp.zeros_like(rec_ref)
    rec_all[n + 1] = jnp.zeros_like(rec_ref)
    tmpl_copy.wait()
    group = 16 if rows % 16 == 0 else 8

    def arrange(g, _):
        for j in range(4):
            turned = jnp.swapaxes(tmpl[pl.ds(g * group, group), :, j * SPAN:(j + 1) * SPAN], 0, 1)
            at = pl.multiple_of(j * rows + g * group, group)
            for c in range(chans):
                lhs[pl.ds(at, group), c * SPAN:(c + 1) * SPAN] = turned[c]
        return 0

    pl.semaphore_wait(barrier, 2 * n - 1)

    def record_copy(i):
        peer = lax.rem(z + i, n)
        return pltpu.make_async_remote_copy(
            src_ref=rec_ref, dst_ref=rec_all.at[z], send_sem=rec_send.at[peer], recv_sem=rec_recv.at[z],
            device_id={"tm": peer, "chan": core}, device_id_type=MESH)

    def record_arrival(i):
        peer = lax.rem(z + i, n)
        return pltpu.make_async_remote_copy(
            src_ref=rec_ref, dst_ref=rec_all.at[peer], send_sem=rec_send.at[peer], recv_sem=rec_recv.at[peer],
            device_id={"tm": peer, "chan": core}, device_id_type=MESH)

    lax.fori_loop(1, n, lambda i, _: (record_copy(i).start(), 0)[1], 0)

    lax.fori_loop(0, rows // group, arrange, 0)

    row = lax.broadcasted_iota(jnp.int32, (chans, 8, SPAN), 1)
    lane = lax.broadcasted_iota(jnp.int32, (chans, 8, SPAN), 2)

    def spread(x):
        return jnp.broadcast_to(x.astype(jnp.float32)[:, None, :], (chans, 8, SPAN))

    def block_at(at):
        lanes = pl.multiple_of(lax.rem(at, slots) * SPAN, SPAN)
        return spread(rec_all[at // slots, :, pl.ds(lanes, SPAN)])

    def shift_rows(now, after):
        y = jnp.where(lane >= row, now, after)
        for bit in (1, 2, 4):
            y = jnp.where((row & bit) > 0, pltpu.roll(y, SPAN - bit, 2), y)
        return y

    def build(pair, hankel, pars=(0, 1)):
        raw = [block_at(2 * pair + i) for i in (0, 1, 2, 2)]
        shifted = [shift_rows(raw[i], raw[i + 1]) for i in range(3)]
        for par in pars:
            now, after = shifted[par], shifted[par + 1]
            for a in range(0, SPAN // 8, 2):
                both = []
                for d in (a, a + 1):
                    y = now
                    if d > 0:
                        y = pltpu.roll(jnp.where(lane >= 8 * d, now, after), SPAN - 8 * d, 2)
                    both.append(y)
                hankel[:, 8 * a:8 * a + 16, par * SPAN:(par + 1) * SPAN] = jnp.concatenate(both, axis=1).astype(jnp.bfloat16)

    def multiply(u, first, second, third):
        depth = chans * SPAN

        def straddle(left, right):
            return jnp.concatenate([left[:, :, SPAN:].reshape(depth, SPAN), right[:, :, :SPAN].reshape(depth, SPAN)], axis=1)

        sides = (first[...].reshape(depth, 2 * SPAN), straddle(first, second),
                 second[...].reshape(depth, 2 * SPAN), straddle(second, third))
        product = None
        for j in range(4):
            term = jnp.dot(lhs[j * rows:(j + 1) * rows, :], sides[j], preferred_element_type=jnp.float32)
            product = term if product is None else product + term
        for par in range(2):
            acc[2 * u + par] = product[:, par * SPAN:(par + 1) * SPAN]

    upper = jnp.where(z >= half, 1, 0)
    turn = (1 - upper) * (2 * n + 2) + upper * (n + 2)

    def pair_at(t):
        wrapped = jnp.where(t >= turn, 1, 0)
        return (1 - wrapped) * (turn - 1 - t) + wrapped * jnp.maximum(2 * n + 1 - (t - turn), 0)

    def chunk_at(t):
        wrapped = jnp.where(t >= turn, 1, 0)
        use = jnp.logical_and(t - wrapped * turn >= 2, jnp.logical_and(t >= 0, t < 2 * n + 2 + 2 * upper))
        return jnp.where(use, pair_at(t), -1)

    def sibling_copy(u):
        return pltpu.make_async_remote_copy(
            src_ref=acc.at[2 * u + 1 - core], dst_ref=sib.at[u],
            send_sem=sib_send.at[u], recv_sem=sib_recv.at[u], device_id=other, device_id_type=MESH)

    def result_copies(u, part, from_core):
        to = {"tm": u // 2, "chan": home}
        block = 2 * (u % 2) + from_core
        slot = part * 4 + block
        return (
            pltpu.make_async_remote_copy(
                src_ref=codes.at[u], dst_ref=codes_in.at[part, block], send_sem=code_send.at[u],
                recv_sem=code_recv.at[slot], device_id=to, device_id_type=MESH),
            pltpu.make_async_remote_copy(
                src_ref=scales.at[u], dst_ref=scales_in.at[part, block], send_sem=scale_send.at[u],
                recv_sem=scale_recv.at[slot], device_id=to, device_id_type=MESH),
        )

    def finish(u, when=True):
        @pl.when(jnp.logical_and(u >= 0, when))
        def _():
            sibling_copy(u).wait_recv()
            keep = jnp.logical_and(u // 2 == z, core == home)
            total = acc[2 * u + core] + sib[u]
            top = jnp.maximum(jnp.max(jnp.abs(total), axis=0, keepdims=True), 1e-37)
            coded = jnp.round((total * (1.0 / top)) * CODES).astype(jnp.int32).astype(jnp.int16)
            scale = jnp.broadcast_to(top * (1.0 / CODES), (8, SPAN))

            @pl.when(keep)
            def _():
                codes_in[own_part, 2 * (u % 2) + core] = coded
                scales_in[own_part, 2 * (u % 2) + core] = scale

            @pl.when(jnp.logical_not(keep))
            def _():
                codes[u] = coded
                scales[u] = scale
                for copy in result_copies(u, own_part, core):
                    copy.start()

    def begin():
        build(pair_at(0), ring[0], (0,))
        build(pair_at(1), ring[1])

    pl.when(upper == 0)(begin)
    lax.fori_loop(1, n, lambda i, _: (record_arrival(i).wait_recv(), 0)[1], 0)
    for part in range(2):
        for b in range(slots):
            piece = rec_all[z + part, :, b * SPAN:(b + 1) * SPAN].astype(jnp.float32)
            e_mine[part * slots + b:part * slots + b + 1, :] = jnp.sum(piece * piece, axis=0, keepdims=True)
    energy_copy = pltpu.make_async_remote_copy(
        src_ref=e_mine, dst_ref=e_sib, send_sem=e_send, recv_sem=e_recv, device_id=other, device_id_type=MESH)
    energy_copy.start()

    pl.when(upper == 1)(begin)


    def step(i, _):
        for r in range(4):
            t = 4 * i + r
            u = chunk_at(t)
            following = pair_at(jnp.minimum(t + 1, 2 * n + 3))

            @pl.when(u >= 0)
            def _():
                build(following, ring[(r + 1) % 4])
                multiply(u, ring[r], ring[(r + 3) % 4], ring[(r + 2) % 4])

            @pl.when(jnp.logical_and(jnp.logical_and(u < 0, t > 0), t + 1 < 2 * n + 2 + 2 * upper))
            def _():
                build(following, ring[(r + 1) % 4])

            @pl.when(u >= 0)
            def _():
                sibling_copy(u).start()

            if r == 2:
                finish(chunk_at(t - 1))
            elif r == 3:
                finish(chunk_at(t - 1))
            else:
                finish(chunk_at(t - 1))
        return 0

    lax.fori_loop(0, (2 * n + 4) // 4, step, 0)
    finish(chunk_at(2 * n + 3))

    energy_copy.wait()
    e = e_mine[...] + e_sib[...]
    i0 = lax.broadcasted_iota(jnp.int32, (SPAN, SPAN), 0)
    i1 = lax.broadcasted_iota(jnp.int32, (SPAN, SPAN), 1)
    dot = functools.partial(jnp.dot, preferred_element_type=jnp.float32, precision=lax.Precision.HIGHEST)
    tails = dot(e, jnp.where(i0 >= i1, 1.0, 0.0))
    heads = dot(e, jnp.where(i0 < i1, 1.0, 0.0))
    sums = jnp.sum(e, axis=1, keepdims=True)
    for b in range(slots):
        energy = tails[b:b + 1] + heads[b + 4:b + 5] + sums[b + 1:b + 2] + sums[b + 2:b + 3] + sums[b + 3:b + 4]
        e_mine[b:b + 1, :] = lax.rsqrt(energy / (2 * chans * 4 * SPAN) + 1e-05)

    def arrival(i, _):
        part, block = i // 4, i % 4
        from_core = block % 2
        source = core * half + part

        @pl.when(jnp.logical_not(jnp.logical_and(source == z, from_core == core)))
        def _():
            for copy in result_copies(block // 2, part, from_core):
                copy.wait_recv()

        return 0

    lax.fori_loop(0, 2 * n, arrival, 0)

    for slot in range(slots):
        at = span_ref[0, slot]
        block = jnp.maximum(at, 0)
        inverse = jnp.where(at >= 0, e_mine[pl.ds(block, 1), :], 0.0)
        for part in range(half):
            values = codes_in[part, block].astype(jnp.int32).astype(jnp.float32)
            scale = scales_in[part, block, 0:1] * inverse
            out_ref[part * rows:(part + 1) * rows, slot * SPAN:(slot + 1) * SPAN] = values * scale

    def drain(u, _):
        sibling_copy(u).wait_send()

        @pl.when(jnp.logical_not(jnp.logical_and(u // 2 == z, core == home)))
        def _():
            for copy in result_copies(u, own_part, core):
                copy.wait_send()

        return 0

    lax.fori_loop(0, 2 * n, drain, 0)
    lax.fori_loop(1, n, lambda i, _: (record_copy(i).wait_send(), 0)[1], 0)


def local(n, record, templates, span_list):
    _, rows, chans, _ = templates.shape
    slots = span_list.shape[1]
    vmem = pl.BlockSpec(memory_space=pltpu.VMEM)
    dma = pltpu.SemaphoreType.DMA
    return pl.pallas_call(
        functools.partial(kernel, n, rows, chans, slots),
        out_shape=pltpu.VMEM((rows * n // 2, slots * SPAN), jnp.float32),
        in_specs=[pl.BlockSpec(memory_space=pltpu.SMEM), vmem, pl.BlockSpec(memory_space=pltpu.HBM)],
        out_specs=vmem,
        scratch_shapes=[
            pltpu.VMEM(templates.shape[1:], jnp.bfloat16),
            pltpu.VMEM((4 * rows, chans * SPAN), jnp.bfloat16),
            pltpu.VMEM((n + 2, chans, record.shape[1]), jnp.bfloat16),
            pltpu.VMEM((chans, SPAN, 2 * SPAN), jnp.bfloat16),
            pltpu.VMEM((chans, SPAN, 2 * SPAN), jnp.bfloat16),
            pltpu.VMEM((chans, SPAN, 2 * SPAN), jnp.bfloat16),
            pltpu.VMEM((chans, SPAN, 2 * SPAN), jnp.bfloat16),
            pltpu.VMEM((4 * n, rows, SPAN), jnp.float32),
            pltpu.VMEM((2 * n, rows, SPAN), jnp.float32),
            pltpu.VMEM((2 * n, rows, SPAN), jnp.int16),
            pltpu.VMEM((2 * n, 8, SPAN), jnp.float32),
            pltpu.VMEM((n // 2, 4, rows, SPAN), jnp.int16),
            pltpu.VMEM((n // 2, 4, 8, SPAN), jnp.float32),
            pltpu.VMEM((8, SPAN), jnp.float32),
            pltpu.VMEM((8, SPAN), jnp.float32),
            dma((n,)), dma((n,)), dma((2 * n,)), dma((2 * n,)), dma((2 * n,)), dma((2 * n,)), dma((2 * n,)), dma((2 * n,)),
            dma, dma, dma,
        ],
        compiler_params=pltpu.CompilerParams(collective_id=0, has_side_effects=True, vmem_limit_bytes=40 * 2**20),
    )(pltpu.with_memory_space_constraint(span_list, pltpu.HBM), pltpu.with_memory_space_constraint(record, pltpu.HBM), pltpu.with_memory_space_constraint(templates, pltpu.HBM))


def solution(mesh):
    in_specs = (P("chan", ("grp", "tm")), P("tmpl", "tm", "chan", None), P(("grp", "tm"), None))
    out_specs = P(("tmpl", "chan"), ("grp", "tm"))
    return jax.shard_map(functools.partial(local, mesh.shape["tm"]), mesh=mesh, in_specs=in_specs, out_specs=out_specs, check_vma=False)
```

```python
import functools

import jax
import jax.numpy as jnp
from jax import lax
from jax.experimental import pallas as pl
from jax.experimental.pallas import tpu as pltpu
from jax.sharding import PartitionSpec as P

SPAN = 128
TAPS = 4
CODES = 32767.0
MESH = pl.DeviceIdType.MESH


def float_chunks(n):
    return (2 * (n // 3) + (1 if n % 3 == 2 else 0) + 1) // 2


def kernel(n, rows, chans, slots, span_ref, rec_ref, tmpl_ref, out_ref, tmpl, lhs, rec_all, span_all, blk, wide, hank_a, hank_b, hank_c, hank_d,
           acc, sib, codes, scales, direct_in, dscale_in, float_in, fscale_in, e_mine, e_sib, own_sem, span_sem, tmpl_sem, rec_send, rec_recv,
           span_send, span_recv, sib_send, sib_recv, code_send, scale_send, side_send, sidescale_send, direct_recv, dscale_recv,
           float_recv, fscale_recv, fwd_send, fwdscale_send, e_send, e_recv):
    z = lax.axis_index("tm")
    core = lax.axis_index("chan")
    half = n // 2
    home = z // half
    own_part = z % half
    other = {"tm": z, "chan": 1 - core}
    hank = (hank_a, hank_b, hank_c, hank_d)
    nf = float_chunks(n)
    chunks = nf + n
    group = 16 if rows % 16 == 0 else 8
    pieces = 3
    share = rows // pieces

    def tmpl_copy(i):
        return pltpu.make_async_copy(tmpl_ref.at[0, pl.ds(i * share, share)], tmpl.at[pl.ds(i * share, share)], tmpl_sem.at[i])

    own_copy = pltpu.make_async_copy(rec_ref, rec_all.at[z], own_sem)
    span_copy = pltpu.make_async_copy(span_ref, span_all.at[z], span_sem)

    barrier = pltpu.get_barrier_semaphore()

    def greet(i, _):
        peer = lax.rem(z + i // 2, n)
        to = lax.rem(core + i % 2, 2)
        pl.semaphore_signal(barrier, inc=1, device_id={"tm": peer, "chan": to}, device_id_type=MESH)
        return 0

    lax.fori_loop(1, 2 * n, greet, 0)
    own_copy.start()
    span_copy.start()
    for i in range(pieces):
        tmpl_copy(i).start()

    def record_copies(i, to):
        peer = lax.rem(z + i, n)
        at = z if to else peer
        target = {"tm": peer, "chan": core}
        return (
            pltpu.make_async_remote_copy(
                src_ref=rec_ref, dst_ref=rec_all.at[at], send_sem=rec_send.at[peer], recv_sem=rec_recv.at[at],
                device_id=target, device_id_type=MESH),
            pltpu.make_async_remote_copy(
                src_ref=span_ref, dst_ref=span_all.at[at], send_sem=span_send.at[peer], recv_sem=span_recv.at[at],
                device_id=target, device_id_type=MESH),
        )

    pl.semaphore_wait(barrier, 2 * n - 1)

    def send_record(i, _):
        for copy in record_copies(i, True):
            copy.start()
        return 0

    lax.fori_loop(1, n, send_record, 0)
    wide_shape = (chans, 16, SPAN)
    rec_all[n] = jnp.zeros(rec_all.shape[1:], jnp.bfloat16)
    for b in range(TAPS + 1):
        wide[n * slots + b] = jnp.zeros(wide_shape, jnp.bfloat16)

    def arrange(g, _):
        for j in range(TAPS):
            turned = jnp.swapaxes(tmpl[pl.ds(g * group, group), :, j * SPAN:(j + 1) * SPAN], 0, 1)
            at = pl.multiple_of(j * rows + g * group, group)
            for c in range(chans):
                lhs[pl.ds(at, group), c * SPAN:(c + 1) * SPAN] = turned[c]
        return 0

    steps = rows // group

    def take(i, _):
        tmpl_copy(i).wait()
        lax.fori_loop(i * (steps // pieces), (i + 1) * (steps // pieces), arrange, 0)
        return 0

    lax.fori_loop(0, pieces, take, 0)

    flip = SPAN - 1 - lax.broadcasted_iota(jnp.int32, (chans, SPAN), 1)

    def widen(shard):
        for b in range(slots):
            x = rec_all[shard, :, b * SPAN:(b + 1) * SPAN].astype(jnp.float32)
            x = jnp.take_along_axis(x, flip, axis=1)
            wide[shard * slots + b] = jnp.broadcast_to(x[:, None, :], wide_shape).astype(jnp.bfloat16)

    own_copy.wait()
    span_copy.wait()
    widen(z)

    def receive_record(i, _):
        for copy in record_copies(i, False):
            copy.wait_recv()
        widen(lax.rem(z + i, n))
        return 0

    lax.fori_loop(1, n, receive_record, 0)

    for f in range(2 * nf):
        def find(i, carry):
            found, seen = carry
            s, q = i // (slots - 2), 2 + i % (slots - 2)
            b = span_all[s, 0, q]
            listed = jnp.where(b >= 0, 1, 0)
            hit = jnp.where(seen == f, listed, 0)
            return found + hit * (s * slots + b), seen + listed

        found, _ = lax.fori_loop(0, n * (slots - 2), find, (jnp.int32(0), jnp.int32(0)))
        blk[f // 2, f % 2] = found

    far_first = jnp.where(z >= half, 0, n - 1)
    stride = jnp.where(z >= half, 1, -1)

    def shard_of(t):
        return far_first + stride * (t - nf)

    def listing(t, _):
        s = shard_of(t)
        for q in range(2):
            blk[t, q] = s * slots + jnp.maximum(span_all[s, 0, q], 0)
        return 0

    lax.fori_loop(nf, chunks, listing, 0)

    reach = (lax.broadcasted_iota(jnp.int32, (16, SPAN), 0) + lax.broadcasted_iota(jnp.int32, (16, SPAN), 1)).astype(jnp.int16)
    reach = jnp.broadcast_to(reach[None], wide_shape)

    def build(t, j):
        for q in range(2):
            at = blk[t, q] + j
            now, after = wide[at], wide[at + 1]
            for a in range(SPAN // 16):
                y = jnp.where(reach < SPAN - 16 * a, now, after)
                hank[j][:, 16 * a:16 * a + 16, q * SPAN:(q + 1) * SPAN] = pltpu.roll(y, 16 * a, 2, stride=1, stride_axis=1)

    def dot(j):
        return jnp.dot(lhs[j * rows:(j + 1) * rows, :], hank[j][...].reshape(chans * SPAN, 2 * SPAN), preferred_element_type=jnp.float32)

    def sibling_copy(t):
        return pltpu.make_async_remote_copy(
            src_ref=acc.at[t, 1 - core], dst_ref=sib.at[t],
            send_sem=sib_send.at[t], recv_sem=sib_recv.at[t], device_id=other, device_id_type=MESH)

    def direct_copies(t, from_core):
        to = {"tm": shard_of(t), "chan": home}
        slot = own_part * 2 + from_core
        return (
            pltpu.make_async_remote_copy(
                src_ref=codes.at[t], dst_ref=direct_in.at[slot], send_sem=code_send.at[t],
                recv_sem=direct_recv.at[slot], device_id=to, device_id_type=MESH),
            pltpu.make_async_remote_copy(
                src_ref=scales.at[t], dst_ref=dscale_in.at[slot], send_sem=scale_send.at[t],
                recv_sem=dscale_recv.at[slot], device_id=to, device_id_type=MESH),
        )

    gate = jnp.where(z < half, half, half - 1)
    is_gate = jnp.logical_or(z == half, z == half - 1)

    def float_copies(t, way):
        peer = jnp.where(way < half, home * half + lax.rem(own_part + way, half), gate)
        slot = own_part * 2 * nf + 2 * t + core
        return (
            pltpu.make_async_remote_copy(
                src_ref=codes.at[t], dst_ref=float_in.at[slot], send_sem=side_send.at[(half + 1) * t + way],
                recv_sem=float_recv.at[slot], device_id={"tm": peer, "chan": home}, device_id_type=MESH),
            pltpu.make_async_remote_copy(
                src_ref=scales.at[t], dst_ref=fscale_in.at[slot], send_sem=sidescale_send.at[(half + 1) * t + way],
                recv_sem=fscale_recv.at[slot], device_id={"tm": peer, "chan": home}, device_id_type=MESH),
        )

    def float_ways(t, started):
        def one(i, _):
            way = half - i

            @pl.when(jnp.logical_or(way > 0, core != home))
            def _():
                for copy in float_copies(t, way):
                    if started:
                        copy.wait_send()
                    else:
                        copy.start()
            return 0

        lax.fori_loop(0, half + 1, one, 0)

    back = SPAN - 1 - lax.broadcasted_iota(jnp.int32, (rows, SPAN), 1)

    def finish(t):
        sibling_copy(t).wait_recv()
        total = acc[t, core] + sib[t]
        total = jnp.take_along_axis(total, back, axis=1)
        top = jnp.maximum(jnp.max(jnp.abs(total), axis=0, keepdims=True), 1e-37)
        coded = jnp.round((total * (1.0 / top)) * CODES).astype(jnp.int32).astype(jnp.int16)
        scale = top * (1.0 / CODES)
        codes[t] = coded
        scales[t] = scale
        direct = t >= nf

        @pl.when(jnp.logical_and(direct, jnp.logical_not(jnp.logical_and(shard_of(t) == z, core == home))))
        def _():
            for copy in direct_copies(t, core):
                copy.start()

        @pl.when(jnp.logical_and(direct, jnp.logical_and(shard_of(t) == z, core == home)))
        def _():
            direct_in[own_part * 2 + core] = coded
            dscale_in[own_part * 2 + core] = scale

        @pl.when(jnp.logical_not(direct))
        def _():
            float_ways(t, False)

            @pl.when(core == home)
            def _():
                float_in[own_part * 2 * nf + 2 * t + core] = coded
                fscale_in[own_part * 2 * nf + 2 * t + core] = scale

    def float_arrival(slot):
        return (
            pltpu.make_async_remote_copy(
                src_ref=float_in.at[slot], dst_ref=float_in.at[slot], send_sem=fwd_send.at[slot],
                recv_sem=float_recv.at[slot], device_id=other, device_id_type=MESH),
            pltpu.make_async_remote_copy(
                src_ref=fscale_in.at[slot], dst_ref=fscale_in.at[slot], send_sem=fwdscale_send.at[slot],
                recv_sem=fscale_recv.at[slot], device_id=other, device_id_type=MESH),
        )

    def forward_copies(slot, step):
        to = {"tm": home * half + lax.rem(own_part + step, half), "chan": core}
        at = slot * half + step
        return (
            pltpu.make_async_remote_copy(
                src_ref=float_in.at[slot], dst_ref=float_in.at[slot], send_sem=fwd_send.at[at],
                recv_sem=float_recv.at[slot], device_id=to, device_id_type=MESH),
            pltpu.make_async_remote_copy(
                src_ref=fscale_in.at[slot], dst_ref=fscale_in.at[slot], send_sem=fwdscale_send.at[at],
                recv_sem=fscale_recv.at[slot], device_id=to, device_id_type=MESH),
        )

    def hand_on(started):
        @pl.when(jnp.logical_and(is_gate, core != home))
        def _():
            def one(slot, _):
                if not started:
                    for copy in float_arrival(slot):
                        copy.wait_recv()

                def on(step, _):
                    for copy in forward_copies(slot, step):
                        if started:
                            copy.wait_send()
                        else:
                            copy.start()
                    return 0

                lax.fori_loop(1, half, on, 0)
                return 0

            lax.fori_loop(0, half * 2 * nf, one, 0)

    energy_copy = pltpu.make_async_remote_copy(
        src_ref=e_mine, dst_ref=e_sib, send_sem=e_send, recv_sem=e_recv, device_id=other, device_id_type=MESH)

    def energies():
        for part in range(2):
            for b in range(slots):
                piece = rec_all[z + part, :, b * SPAN:(b + 1) * SPAN].astype(jnp.float32)
                e_mine[part * slots + b:part * slots + b + 1, :] = jnp.sum(piece * piece, axis=0, keepdims=True)
        energy_copy.start()

    def inverses():
        energy_copy.wait()
        e = e_mine[...] + e_sib[...]
        i0 = lax.broadcasted_iota(jnp.int32, (SPAN, SPAN), 0)
        i1 = lax.broadcasted_iota(jnp.int32, (SPAN, SPAN), 1)
        exact = functools.partial(jnp.dot, preferred_element_type=jnp.float32, precision=lax.Precision.HIGHEST)
        tails = exact(e, jnp.where(i0 >= i1, 1.0, 0.0))
        heads = exact(e, jnp.where(i0 < i1, 1.0, 0.0))
        sums = jnp.sum(e, axis=1, keepdims=True)
        for b in range(slots):
            energy = tails[b:b + 1] + heads[b + 4:b + 5] + sums[b + 1:b + 2] + sums[b + 2:b + 3] + sums[b + 3:b + 4]
            e_mine[b:b + 1, :] = lax.rsqrt(energy / (2 * chans * TAPS * SPAN) + 1e-05)

    build(0, 0)
    build(0, 1)

    def step(t, _):
        following = jnp.minimum(t + 1, chunks - 1)
        build(t, 2)
        product = dot(0)
        build(t, 3)
        product += dot(1)
        build(following, 0)
        product += dot(2)
        acc[t] = jnp.stack([product[:, :SPAN], product[:, SPAN:]])

        @pl.when(t > 0)
        def _():
            finish(t - 1)

        pl.when(t == 1)(energies)
        pl.when(t == chunks - 1)(inverses)
        build(following, 1)
        product = dot(3)
        for q in range(2):
            acc[t, q] += product[:, q * SPAN:(q + 1) * SPAN]
        sibling_copy(t).start()
        return 0

    lax.fori_loop(0, chunks, step, 0)
    hand_on(False)
    finish(chunks - 1)

    def put(part, slot, values, scale, inverse):
        out_ref[part * rows:(part + 1) * rows, slot * SPAN:(slot + 1) * SPAN] = values.astype(jnp.int32).astype(jnp.float32) * (scale * inverse)

    at = [span_all[z, 0, q] for q in range(slots)]
    inverse = [jnp.where(b >= 0, e_mine[pl.ds(jnp.maximum(b, 0), 1), :], 0.0) for b in at]
    for part in range(half):
        source = core * half + part
        for q in range(2):
            @pl.when(jnp.logical_not(jnp.logical_and(source == z, core == q)))
            def _():
                slot = part * 2 + q
                pltpu.make_async_remote_copy(
                    src_ref=codes.at[0], dst_ref=direct_in.at[slot], send_sem=code_send.at[0],
                    recv_sem=direct_recv.at[slot], device_id=other, device_id_type=MESH).wait_recv()
                pltpu.make_async_remote_copy(
                    src_ref=scales.at[0], dst_ref=dscale_in.at[slot], send_sem=scale_send.at[0],
                    recv_sem=dscale_recv.at[slot], device_id=other, device_id_type=MESH).wait_recv()

            put(part, q, direct_in[part * 2 + q], dscale_in[part * 2 + q], inverse[q])

    @pl.when(jnp.logical_not(jnp.logical_and(is_gate, core != home)))
    def _():
        def one(slot, _):
            part, f = slot // (2 * nf), lax.rem(slot, 2 * nf)

            @pl.when(jnp.logical_not(jnp.logical_and(core == home, jnp.logical_and(part == own_part, lax.rem(f, 2) == core))))
            def _():
                for copy in float_arrival(slot):
                    copy.wait_recv()
            return 0

        lax.fori_loop(0, half * 2 * nf, one, 0)

    def earlier(i, count):
        before = jnp.where(i // (slots - 2) < z, 1, 0)
        return count + before * jnp.where(span_all[i // (slots - 2), 0, 2 + i % (slots - 2)] >= 0, 1, 0)

    first = lax.fori_loop(0, n * (slots - 2), earlier, jnp.int32(0))
    for q in range(2, slots):
        f = jnp.minimum(first + q - 2, 2 * nf - 1)
        for part in range(half):
            put(part, q, float_in[part * 2 * nf + f], fscale_in[part * 2 * nf + f], inverse[q])

    def drain(t, _):
        sibling_copy(t).wait_send()

        @pl.when(jnp.logical_and(t >= nf, jnp.logical_not(jnp.logical_and(shard_of(t) == z, core == home))))
        def _():
            for copy in direct_copies(t, core):
                copy.wait_send()

        @pl.when(t < nf)
        def _():
            float_ways(t, True)

        return 0

    lax.fori_loop(0, chunks, drain, 0)
    hand_on(True)

    def sent(i, _):
        for copy in record_copies(i, True):
            copy.wait_send()
        return 0

    lax.fori_loop(1, n, sent, 0)


def local(n, record, templates, span_list):
    _, rows, chans, _ = templates.shape
    slots = span_list.shape[1]
    nf = float_chunks(n)
    chunks = nf + n
    half = n // 2
    hbm = pl.BlockSpec(memory_space=pltpu.HBM)
    dma = pltpu.SemaphoreType.DMA
    hank = pltpu.VMEM((chans, SPAN, 2 * SPAN), jnp.bfloat16)
    return pl.pallas_call(
        functools.partial(kernel, n, rows, chans, slots),
        out_shape=pltpu.VMEM((rows * half, slots * SPAN), jnp.float32),
        in_specs=[hbm, hbm, hbm],
        out_specs=pl.BlockSpec(memory_space=pltpu.VMEM),
        scratch_shapes=[
            pltpu.VMEM(templates.shape[1:], jnp.bfloat16),
            pltpu.VMEM((TAPS * rows, chans * SPAN), jnp.bfloat16),
            pltpu.VMEM((n + 1, chans, record.shape[1]), jnp.bfloat16),
            pltpu.SMEM((n, 1, slots), jnp.int32),
            pltpu.SMEM((chunks, 2), jnp.int32),
            pltpu.VMEM((n * slots + TAPS + 1, chans, 16, SPAN), jnp.bfloat16),
            hank, hank, hank, hank,
            pltpu.VMEM((chunks, 2, rows, SPAN), jnp.float32),
            pltpu.VMEM((chunks, rows, SPAN), jnp.float32),
            pltpu.VMEM((chunks, rows, SPAN), jnp.int16),
            pltpu.VMEM((chunks, 1, SPAN), jnp.float32),
            pltpu.VMEM((half * 2, rows, SPAN), jnp.int16),
            pltpu.VMEM((half * 2, 1, SPAN), jnp.float32),
            pltpu.VMEM((half * 2 * nf, rows, SPAN), jnp.int16),
            pltpu.VMEM((half * 2 * nf, 1, SPAN), jnp.float32),
            pltpu.VMEM((8, SPAN), jnp.float32),
            pltpu.VMEM((8, SPAN), jnp.float32),
            dma, dma, dma((3,)), dma((n,)), dma((n,)), dma((n,)), dma((n,)),
            dma((chunks,)), dma((chunks,)), dma((chunks,)), dma((chunks,)), dma(((half + 1) * nf,)), dma(((half + 1) * nf,)),
            dma((half * 2,)), dma((half * 2,)), dma((half * 2 * nf,)), dma((half * 2 * nf,)),
            dma((half * half * 2 * nf,)), dma((half * half * 2 * nf,)), dma, dma,
        ],
        compiler_params=pltpu.CompilerParams(collective_id=0, has_side_effects=True, vmem_limit_bytes=40 * 2**20),
    )(*(pltpu.with_memory_space_constraint(x, pltpu.HBM) for x in (span_list, record, templates)))


def solution(mesh):
    in_specs = (P("chan", ("grp", "tm")), P("tmpl", "tm", "chan", None), P(("grp", "tm"), None))
    out_specs = P(("tmpl", "chan"), ("grp", "tm"))
    return jax.shard_map(functools.partial(local, mesh.shape["tm"]), mesh=mesh, in_specs=in_specs, out_specs=out_specs, check_vma=False)
```

```python
import functools

import jax
import jax.numpy as jnp
from jax import lax
from jax.experimental import pallas as pl
from jax.experimental.pallas import tpu as pltpu
from jax.sharding import PartitionSpec as P

SPAN = 128
TAPS = 4
CODES = 32767.0
MESH = pl.DeviceIdType.MESH


def float_chunks(n):
    return (2 * (n // 3) + (1 if n % 3 == 2 else 0) + 1) // 2


def kernel(n, rows, chans, slots, span_ref, rec_ref, tmpl_ref, out_ref, tmpl, lhs, rec_all, span_all, blk, wide, hank_a, hank_b, hank_c, hank_d,
           acc, sib, codes, scales, direct_in, dscale_in, float_in, fscale_in, e_mine, e_sib, own_sem, span_sem, tmpl_sem, rec_send, rec_recv,
           span_send, span_recv, sib_send, sib_recv, code_send, scale_send, side_send, sidescale_send, direct_recv, dscale_recv,
           float_recv, fscale_recv, fwd_send, fwdscale_send, e_send, e_recv):
    z = lax.axis_index("tm")
    core = lax.axis_index("chan")
    half = n // 2
    home = z // half
    own_part = z % half
    other = {"tm": z, "chan": 1 - core}
    hank = (hank_a, hank_b, hank_c, hank_d)
    nf = float_chunks(n)
    chunks = nf + n
    group = 16 if rows % 16 == 0 else 8
    pieces = 3
    share = rows // pieces

    def tmpl_copy(i):
        return pltpu.make_async_copy(tmpl_ref.at[0, pl.ds(i * share, share)], tmpl.at[pl.ds(i * share, share)], tmpl_sem.at[i])

    own_copy = pltpu.make_async_copy(rec_ref, rec_all.at[z], own_sem)
    span_copy = pltpu.make_async_copy(span_ref, span_all.at[z], span_sem)

    barrier = pltpu.get_barrier_semaphore()

    def greet(i, _):
        peer = lax.rem(z + i // 2, n)
        to = lax.rem(core + i % 2, 2)
        pl.semaphore_signal(barrier, inc=1, device_id={"tm": peer, "chan": to}, device_id_type=MESH)
        return 0

    lax.fori_loop(1, 2 * n, greet, 0)
    own_copy.start()
    span_copy.start()
    for i in range(pieces):
        tmpl_copy(i).start()

    def record_copies(i, to):
        peer = lax.rem(z + i, n)
        at = z if to else peer
        target = {"tm": peer, "chan": core}
        return (
            pltpu.make_async_remote_copy(
                src_ref=rec_ref, dst_ref=rec_all.at[at], send_sem=rec_send.at[peer], recv_sem=rec_recv.at[at],
                device_id=target, device_id_type=MESH),
            pltpu.make_async_remote_copy(
                src_ref=span_ref, dst_ref=span_all.at[at], send_sem=span_send.at[peer], recv_sem=span_recv.at[at],
                device_id=target, device_id_type=MESH),
        )

    pl.semaphore_wait(barrier, 2 * n - 1)

    def send_record(i, _):
        for copy in record_copies(i, True):
            copy.start()
        return 0

    lax.fori_loop(1, n, send_record, 0)
    wide_shape = (chans, 16, SPAN)
    rec_all[n] = jnp.zeros(rec_all.shape[1:], jnp.bfloat16)
    for b in range(TAPS + 1):
        wide[n * slots + b] = jnp.zeros(wide_shape, jnp.bfloat16)

    def arrange(g, _):
        for j in range(TAPS):
            turned = jnp.swapaxes(tmpl[pl.ds(g * group, group), :, j * SPAN:(j + 1) * SPAN], 0, 1)
            at = pl.multiple_of(j * rows + g * group, group)
            for c in range(chans):
                lhs[pl.ds(at, group), c * SPAN:(c + 1) * SPAN] = turned[c]
        return 0

    steps = rows // group

    def take(i, _):
        tmpl_copy(i).wait()
        lax.fori_loop(i * (steps // pieces), (i + 1) * (steps // pieces), arrange, 0)
        return 0

    lax.fori_loop(0, pieces, take, 0)

    flip = SPAN - 1 - lax.broadcasted_iota(jnp.int32, (chans, SPAN), 1)

    def widen(shard):
        for b in range(slots):
            x = rec_all[shard, :, b * SPAN:(b + 1) * SPAN].astype(jnp.float32)
            x = jnp.take_along_axis(x, flip, axis=1)
            wide[shard * slots + b] = jnp.broadcast_to(x[:, None, :], wide_shape).astype(jnp.bfloat16)

    own_copy.wait()
    span_copy.wait()
    widen(z)

    def receive_record(i, _):
        for copy in record_copies(i, False):
            copy.wait_recv()
        widen(lax.rem(z + i, n))
        return 0

    lax.fori_loop(1, n, receive_record, 0)

    for f in range(2 * nf):
        def find(i, carry):
            found, seen = carry
            s, q = i // (slots - 2), 2 + i % (slots - 2)
            b = span_all[s, 0, q]
            listed = jnp.where(b >= 0, 1, 0)
            hit = jnp.where(seen == f, listed, 0)
            return found + hit * (s * slots + b), seen + listed

        found, _ = lax.fori_loop(0, n * (slots - 2), find, (jnp.int32(0), jnp.int32(0)))
        blk[f // 2, f % 2] = found

    def shard_of(t):
        k = t - nf
        across = jnp.where(z >= half, k, n - 1 - k)
        along = home * half + lax.rem(own_part + 1 + k, half)
        return jnp.where(k < half, across, along)

    def listing(t, _):
        s = shard_of(t)
        for q in range(2):
            blk[t, q] = s * slots + jnp.maximum(span_all[s, 0, q], 0)
        return 0

    lax.fori_loop(nf, chunks, listing, 0)

    reach = (lax.broadcasted_iota(jnp.int32, (16, SPAN), 0) + lax.broadcasted_iota(jnp.int32, (16, SPAN), 1)).astype(jnp.int16)
    reach = jnp.broadcast_to(reach[None], wide_shape)

    def build(t, j):
        for q in range(2):
            at = blk[t, q] + j
            now, after = wide[at], wide[at + 1]
            for a in range(SPAN // 16):
                y = jnp.where(reach < SPAN - 16 * a, now, after)
                hank[j][:, 16 * a:16 * a + 16, q * SPAN:(q + 1) * SPAN] = pltpu.roll(y, 16 * a, 2, stride=1, stride_axis=1)

    def dot(j):
        return jnp.dot(lhs[j * rows:(j + 1) * rows, :], hank[j][...].reshape(chans * SPAN, 2 * SPAN), preferred_element_type=jnp.float32)

    def sibling_copy(t):
        return pltpu.make_async_remote_copy(
            src_ref=acc.at[t, 1 - core], dst_ref=sib.at[t],
            send_sem=sib_send.at[t], recv_sem=sib_recv.at[t], device_id=other, device_id_type=MESH)

    def direct_copies(t, from_core):
        to = {"tm": shard_of(t), "chan": home}
        slot = own_part * 2 + from_core
        return (
            pltpu.make_async_remote_copy(
                src_ref=codes.at[t], dst_ref=direct_in.at[slot], send_sem=code_send.at[t],
                recv_sem=direct_recv.at[slot], device_id=to, device_id_type=MESH),
            pltpu.make_async_remote_copy(
                src_ref=scales.at[t], dst_ref=dscale_in.at[slot], send_sem=scale_send.at[t],
                recv_sem=dscale_recv.at[slot], device_id=to, device_id_type=MESH),
        )

    gate = jnp.where(z < half, half, half - 1)
    is_gate = jnp.logical_or(z == half, z == half - 1)

    def float_copies(t, way):
        peer = jnp.where(way < half, home * half + lax.rem(own_part + way, half), gate)
        slot = own_part * 2 * nf + 2 * t + core
        return (
            pltpu.make_async_remote_copy(
                src_ref=codes.at[t], dst_ref=float_in.at[slot], send_sem=side_send.at[(half + 1) * t + way],
                recv_sem=float_recv.at[slot], device_id={"tm": peer, "chan": home}, device_id_type=MESH),
            pltpu.make_async_remote_copy(
                src_ref=scales.at[t], dst_ref=fscale_in.at[slot], send_sem=sidescale_send.at[(half + 1) * t + way],
                recv_sem=fscale_recv.at[slot], device_id={"tm": peer, "chan": home}, device_id_type=MESH),
        )

    def float_ways(t, started):
        def one(i, _):
            way = half - i

            @pl.when(jnp.logical_or(way > 0, core != home))
            def _():
                for copy in float_copies(t, way):
                    if started:
                        copy.wait_send()
                    else:
                        copy.start()
            return 0

        lax.fori_loop(0, half + 1, one, 0)

    back = SPAN - 1 - lax.broadcasted_iota(jnp.int32, (rows, SPAN), 1)

    def finish(t):
        sibling_copy(t).wait_recv()
        total = acc[t, core] + sib[t]
        total = jnp.take_along_axis(total, back, axis=1)
        top = jnp.maximum(jnp.max(jnp.abs(total), axis=0, keepdims=True), 1e-37)
        coded = jnp.round((total * (1.0 / top)) * CODES).astype(jnp.int32).astype(jnp.int16)
        scale = top * (1.0 / CODES)
        codes[t] = coded
        scales[t] = scale
        direct = t >= nf

        @pl.when(jnp.logical_and(direct, jnp.logical_not(jnp.logical_and(shard_of(t) == z, core == home))))
        def _():
            for copy in direct_copies(t, core):
                copy.start()

        @pl.when(jnp.logical_and(direct, jnp.logical_and(shard_of(t) == z, core == home)))
        def _():
            direct_in[own_part * 2 + core] = coded
            dscale_in[own_part * 2 + core] = scale

        @pl.when(jnp.logical_not(direct))
        def _():
            float_ways(t, False)

            @pl.when(core == home)
            def _():
                float_in[own_part * 2 * nf + 2 * t + core] = coded
                fscale_in[own_part * 2 * nf + 2 * t + core] = scale

    def float_arrival(slot):
        return (
            pltpu.make_async_remote_copy(
                src_ref=float_in.at[slot], dst_ref=float_in.at[slot], send_sem=fwd_send.at[slot],
                recv_sem=float_recv.at[slot], device_id=other, device_id_type=MESH),
            pltpu.make_async_remote_copy(
                src_ref=fscale_in.at[slot], dst_ref=fscale_in.at[slot], send_sem=fwdscale_send.at[slot],
                recv_sem=fscale_recv.at[slot], device_id=other, device_id_type=MESH),
        )

    def forward_copies(slot, step):
        to = {"tm": home * half + lax.rem(own_part + step, half), "chan": core}
        at = slot * half + step
        return (
            pltpu.make_async_remote_copy(
                src_ref=float_in.at[slot], dst_ref=float_in.at[slot], send_sem=fwd_send.at[at],
                recv_sem=float_recv.at[slot], device_id=to, device_id_type=MESH),
            pltpu.make_async_remote_copy(
                src_ref=fscale_in.at[slot], dst_ref=fscale_in.at[slot], send_sem=fwdscale_send.at[at],
                recv_sem=fscale_recv.at[slot], device_id=to, device_id_type=MESH),
        )

    def hand_on(started):
        @pl.when(jnp.logical_and(is_gate, core != home))
        def _():
            def one(slot, _):
                if not started:
                    for copy in float_arrival(slot):
                        copy.wait_recv()

                def on(step, _):
                    for copy in forward_copies(slot, step):
                        if started:
                            copy.wait_send()
                        else:
                            copy.start()
                    return 0

                lax.fori_loop(1, half, on, 0)
                return 0

            lax.fori_loop(0, half * 2 * nf, one, 0)

    energy_copy = pltpu.make_async_remote_copy(
        src_ref=e_mine, dst_ref=e_sib, send_sem=e_send, recv_sem=e_recv, device_id=other, device_id_type=MESH)

    def energies():
        for part in range(2):
            for b in range(slots):
                piece = rec_all[z + part, :, b * SPAN:(b + 1) * SPAN].astype(jnp.float32)
                e_mine[part * slots + b:part * slots + b + 1, :] = jnp.sum(piece * piece, axis=0, keepdims=True)
        energy_copy.start()

    def inverses():
        energy_copy.wait()
        e = e_mine[...] + e_sib[...]
        i0 = lax.broadcasted_iota(jnp.int32, (SPAN, SPAN), 0)
        i1 = lax.broadcasted_iota(jnp.int32, (SPAN, SPAN), 1)
        exact = functools.partial(jnp.dot, preferred_element_type=jnp.float32, precision=lax.Precision.HIGHEST)
        tails = exact(e, jnp.where(i0 >= i1, 1.0, 0.0))
        heads = exact(e, jnp.where(i0 < i1, 1.0, 0.0))
        sums = jnp.sum(e, axis=1, keepdims=True)
        for b in range(slots):
            energy = tails[b:b + 1] + heads[b + 4:b + 5] + sums[b + 1:b + 2] + sums[b + 2:b + 3] + sums[b + 3:b + 4]
            e_mine[b:b + 1, :] = lax.rsqrt(energy / (2 * chans * TAPS * SPAN) + 1e-05)

    build(0, 0)
    build(0, 1)

    def step(t, _):
        following = jnp.minimum(t + 1, chunks - 1)
        build(t, 2)
        product = dot(0)
        build(t, 3)
        product += dot(1)
        build(following, 0)
        product += dot(2)
        build(following, 1)
        product += dot(3)
        acc[t] = jnp.stack([product[:, :SPAN], product[:, SPAN:]])
        sibling_copy(t).start()

        @pl.when(t > 0)
        def _():
            finish(t - 1)

        return 0

    lax.fori_loop(0, chunks, step, 0)
    energies()
    finish(chunks - 1)
    hand_on(False)
    inverses()

    def put(part, slot, values, scale, inverse):
        out_ref[part * rows:(part + 1) * rows, slot * SPAN:(slot + 1) * SPAN] = values.astype(jnp.int32).astype(jnp.float32) * (scale * inverse)

    at = [span_all[z, 0, q] for q in range(slots)]
    inverse = [jnp.where(b >= 0, e_mine[pl.ds(jnp.maximum(b, 0), 1), :], 0.0) for b in at]
    for part in range(half):
        source = core * half + part
        for q in range(2):
            @pl.when(jnp.logical_not(jnp.logical_and(source == z, core == q)))
            def _():
                slot = part * 2 + q
                pltpu.make_async_remote_copy(
                    src_ref=codes.at[0], dst_ref=direct_in.at[slot], send_sem=code_send.at[0],
                    recv_sem=direct_recv.at[slot], device_id=other, device_id_type=MESH).wait_recv()
                pltpu.make_async_remote_copy(
                    src_ref=scales.at[0], dst_ref=dscale_in.at[slot], send_sem=scale_send.at[0],
                    recv_sem=dscale_recv.at[slot], device_id=other, device_id_type=MESH).wait_recv()

            put(part, q, direct_in[part * 2 + q], dscale_in[part * 2 + q], inverse[q])

    @pl.when(jnp.logical_not(jnp.logical_and(is_gate, core != home)))
    def _():
        def one(slot, _):
            part, f = slot // (2 * nf), lax.rem(slot, 2 * nf)

            @pl.when(jnp.logical_not(jnp.logical_and(core == home, jnp.logical_and(part == own_part, lax.rem(f, 2) == core))))
            def _():
                for copy in float_arrival(slot):
                    copy.wait_recv()
            return 0

        lax.fori_loop(0, half * 2 * nf, one, 0)

    def earlier(i, count):
        before = jnp.where(i // (slots - 2) < z, 1, 0)
        return count + before * jnp.where(span_all[i // (slots - 2), 0, 2 + i % (slots - 2)] >= 0, 1, 0)

    first = lax.fori_loop(0, n * (slots - 2), earlier, jnp.int32(0))
    for q in range(2, slots):
        f = jnp.minimum(first + q - 2, 2 * nf - 1)
        for part in range(half):
            put(part, q, float_in[part * 2 * nf + f], fscale_in[part * 2 * nf + f], inverse[q])

    def drain(t, _):
        sibling_copy(t).wait_send()

        @pl.when(jnp.logical_and(t >= nf, jnp.logical_not(jnp.logical_and(shard_of(t) == z, core == home))))
        def _():
            for copy in direct_copies(t, core):
                copy.wait_send()

        @pl.when(t < nf)
        def _():
            float_ways(t, True)

        return 0

    lax.fori_loop(0, chunks, drain, 0)
    hand_on(True)

    def sent(i, _):
        for copy in record_copies(i, True):
            copy.wait_send()
        return 0

    lax.fori_loop(1, n, sent, 0)


def local(n, record, templates, span_list):
    _, rows, chans, _ = templates.shape
    slots = span_list.shape[1]
    nf = float_chunks(n)
    chunks = nf + n
    half = n // 2
    hbm = pl.BlockSpec(memory_space=pltpu.HBM)
    dma = pltpu.SemaphoreType.DMA
    hank = pltpu.VMEM((chans, SPAN, 2 * SPAN), jnp.bfloat16)
    return pl.pallas_call(
        functools.partial(kernel, n, rows, chans, slots),
        out_shape=pltpu.VMEM((rows * half, slots * SPAN), jnp.float32),
        in_specs=[hbm, hbm, hbm],
        out_specs=pl.BlockSpec(memory_space=pltpu.VMEM),
        scratch_shapes=[
            pltpu.VMEM(templates.shape[1:], jnp.bfloat16),
            pltpu.VMEM((TAPS * rows, chans * SPAN), jnp.bfloat16),
            pltpu.VMEM((n + 1, chans, record.shape[1]), jnp.bfloat16),
            pltpu.SMEM((n, 1, slots), jnp.int32),
            pltpu.SMEM((chunks, 2), jnp.int32),
            pltpu.VMEM((n * slots + TAPS + 1, chans, 16, SPAN), jnp.bfloat16),
            hank, hank, hank, hank,
            pltpu.VMEM((chunks, 2, rows, SPAN), jnp.float32),
            pltpu.VMEM((chunks, rows, SPAN), jnp.float32),
            pltpu.VMEM((chunks, rows, SPAN), jnp.int16),
            pltpu.VMEM((chunks, 1, SPAN), jnp.float32),
            pltpu.VMEM((half * 2, rows, SPAN), jnp.int16),
            pltpu.VMEM((half * 2, 1, SPAN), jnp.float32),
            pltpu.VMEM((half * 2 * nf, rows, SPAN), jnp.int16),
            pltpu.VMEM((half * 2 * nf, 1, SPAN), jnp.float32),
            pltpu.VMEM((8, SPAN), jnp.float32),
            pltpu.VMEM((8, SPAN), jnp.float32),
            dma, dma, dma((3,)), dma((n,)), dma((n,)), dma((n,)), dma((n,)),
            dma((chunks,)), dma((chunks,)), dma((chunks,)), dma((chunks,)), dma(((half + 1) * nf,)), dma(((half + 1) * nf,)),
            dma((half * 2,)), dma((half * 2,)), dma((half * 2 * nf,)), dma((half * 2 * nf,)),
            dma((half * half * 2 * nf,)), dma((half * half * 2 * nf,)), dma, dma,
        ],
        compiler_params=pltpu.CompilerParams(collective_id=0, has_side_effects=True, vmem_limit_bytes=40 * 2**20),
    )(*(pltpu.with_memory_space_constraint(x, pltpu.HBM) for x in (span_list, record, templates)))


def solution(mesh):
    in_specs = (P("chan", ("grp", "tm")), P("tmpl", "tm", "chan", None), P(("grp", "tm"), None))
    out_specs = P(("tmpl", "chan"), ("grp", "tm"))
    return jax.shard_map(functools.partial(local, mesh.shape["tm"]), mesh=mesh, in_specs=in_specs, out_specs=out_specs, check_vma=False)
```

```python
import functools

import jax
import jax.numpy as jnp
from jax import lax
from jax.experimental import pallas as pl
from jax.experimental.pallas import tpu as pltpu
from jax.sharding import PartitionSpec as P

SPAN = 128
TAPS = 4
CODES = 32767.0
MESH = pl.DeviceIdType.MESH


def float_chunks(n):
    return (2 * (n // 3) + (1 if n % 3 == 2 else 0) + 1) // 2


def kernel(n, rows, chans, slots, span_ref, rec_ref, tmpl_ref, out_ref, tmpl, lhs, rec_all, span_all, blk, wide, hank_a, hank_b, hank_c, hank_d,
           acc, sib, codes, scales, direct_in, dscale_in, float_in, fscale_in, e_mine, e_sib, own_sem, span_sem, tmpl_sem, rec_send, rec_recv,
           span_send, span_recv, sib_send, sib_recv, code_send, scale_send, side_send, sidescale_send, direct_recv, dscale_recv,
           float_recv, fscale_recv, fwd_send, fwdscale_send, e_send, e_recv):
    z = lax.axis_index("tm")
    core = lax.axis_index("chan")
    half = n // 2
    home = z // half
    own_part = z % half
    other = {"tm": z, "chan": 1 - core}
    hank = (hank_a, hank_b, hank_c, hank_d)
    nf = float_chunks(n)
    chunks = nf + n
    group = 16 if rows % 16 == 0 else 8
    pieces = 3
    share = rows // pieces

    def tmpl_copy(i):
        return pltpu.make_async_copy(tmpl_ref.at[0, pl.ds(i * share, share)], tmpl.at[pl.ds(i * share, share)], tmpl_sem.at[i])

    own_copy = pltpu.make_async_copy(rec_ref, rec_all.at[z], own_sem)
    span_copy = pltpu.make_async_copy(span_ref, span_all.at[z], span_sem)

    barrier = pltpu.get_barrier_semaphore()

    def greet(i, _):
        peer = lax.rem(z + i // 2, n)
        to = lax.rem(core + i % 2, 2)
        pl.semaphore_signal(barrier, inc=1, device_id={"tm": peer, "chan": to}, device_id_type=MESH)
        return 0

    lax.fori_loop(1, 2 * n, greet, 0)
    own_copy.start()
    span_copy.start()
    for i in range(pieces):
        tmpl_copy(i).start()

    def record_copies(i, to):
        peer = lax.rem(z + i, n)
        at = z if to else peer
        target = {"tm": peer, "chan": core}
        return (
            pltpu.make_async_remote_copy(
                src_ref=rec_ref, dst_ref=rec_all.at[at], send_sem=rec_send.at[peer], recv_sem=rec_recv.at[at],
                device_id=target, device_id_type=MESH),
            pltpu.make_async_remote_copy(
                src_ref=span_ref, dst_ref=span_all.at[at], send_sem=span_send.at[peer], recv_sem=span_recv.at[at],
                device_id=target, device_id_type=MESH),
        )

    pl.semaphore_wait(barrier, 2 * n - 1)

    def send_record(i, _):
        for copy in record_copies(i, True):
            copy.start()
        return 0

    lax.fori_loop(1, n, send_record, 0)
    wide_shape = (chans, 16, SPAN)
    rec_all[n] = jnp.zeros(rec_all.shape[1:], jnp.bfloat16)
    for b in range(TAPS + 1):
        wide[n * slots + b] = jnp.zeros(wide_shape, jnp.bfloat16)

    def arrange(g, _):
        for j in range(TAPS):
            turned = jnp.swapaxes(tmpl[pl.ds(g * group, group), :, j * SPAN:(j + 1) * SPAN], 0, 1)
            at = pl.multiple_of(j * rows + g * group, group)
            for c in range(chans):
                lhs[pl.ds(at, group), c * SPAN:(c + 1) * SPAN] = turned[c]
        return 0

    steps = rows // group

    def take(i, _):
        tmpl_copy(i).wait()
        lax.fori_loop(i * (steps // pieces), (i + 1) * (steps // pieces), arrange, 0)
        return 0

    lax.fori_loop(0, pieces, take, 0)

    flip = SPAN - 1 - lax.broadcasted_iota(jnp.int32, (chans, SPAN), 1)

    def widen(shard):
        for b in range(slots):
            x = rec_all[shard, :, b * SPAN:(b + 1) * SPAN].astype(jnp.float32)
            x = jnp.take_along_axis(x, flip, axis=1)
            wide[shard * slots + b] = jnp.broadcast_to(x[:, None, :], wide_shape).astype(jnp.bfloat16)

    own_copy.wait()
    span_copy.wait()
    widen(z)

    def receive_record(i, _):
        for copy in record_copies(i, False):
            copy.wait_recv()
        widen(lax.rem(z + i, n))
        return 0

    lax.fori_loop(1, n, receive_record, 0)

    found, seen = [jnp.int32(0)] * (2 * nf), jnp.int32(0)
    for i in range(n * (slots - 2)):
        s, q = i // (slots - 2), 2 + i % (slots - 2)
        b = span_all[s, 0, q]
        listed = jnp.where(b >= 0, 1, 0)
        found = [c + jnp.where(seen == f, listed, 0) * (s * slots + b) for f, c in enumerate(found)]
        seen = seen + listed
    for f in range(2 * nf):
        blk[f // 2, f % 2] = found[f]

    def shard_of(t):
        k = t - nf
        across = jnp.where(z >= half, k, n - 1 - k)
        along = home * half + lax.rem(own_part + 1 + k, half)
        return jnp.where(k < half, across, along)

    def listing(t, _):
        s = shard_of(t)
        for q in range(2):
            blk[t, q] = s * slots + jnp.maximum(span_all[s, 0, q], 0)
        return 0

    lax.fori_loop(nf, chunks, listing, 0)

    reach = (lax.broadcasted_iota(jnp.int32, (16, SPAN), 0) + lax.broadcasted_iota(jnp.int32, (16, SPAN), 1)).astype(jnp.int16)
    reach = jnp.broadcast_to(reach[None], wide_shape)

    def build(t, j):
        for q in range(2):
            at = blk[t, q] + j
            now, after = wide[at], wide[at + 1]
            for a in range(SPAN // 16):
                y = jnp.where(reach < SPAN - 16 * a, now, after)
                hank[j][:, 16 * a:16 * a + 16, q * SPAN:(q + 1) * SPAN] = pltpu.roll(y, 16 * a, 2, stride=1, stride_axis=1)

    def dot(j):
        return jnp.dot(lhs[j * rows:(j + 1) * rows, :], hank[j][...].reshape(chans * SPAN, 2 * SPAN), preferred_element_type=jnp.float32)

    def sibling_copy(t):
        return pltpu.make_async_remote_copy(
            src_ref=acc.at[t, 1 - core], dst_ref=sib.at[t],
            send_sem=sib_send.at[t], recv_sem=sib_recv.at[t], device_id=other, device_id_type=MESH)

    def direct_copies(t, from_core):
        to = {"tm": shard_of(t), "chan": home}
        slot = own_part * 2 + from_core
        return (
            pltpu.make_async_remote_copy(
                src_ref=codes.at[t], dst_ref=direct_in.at[slot], send_sem=code_send.at[t],
                recv_sem=direct_recv.at[slot], device_id=to, device_id_type=MESH),
            pltpu.make_async_remote_copy(
                src_ref=scales.at[t], dst_ref=dscale_in.at[slot], send_sem=scale_send.at[t],
                recv_sem=dscale_recv.at[slot], device_id=to, device_id_type=MESH),
        )

    gate = jnp.where(z < half, half, half - 1)
    is_gate = jnp.logical_or(z == half, z == half - 1)

    def float_copies(t, way):
        peer = jnp.where(way < half, home * half + lax.rem(own_part + way, half), gate)
        slot = own_part * 2 * nf + 2 * t + core
        return (
            pltpu.make_async_remote_copy(
                src_ref=codes.at[t], dst_ref=float_in.at[slot], send_sem=side_send.at[(half + 1) * t + way],
                recv_sem=float_recv.at[slot], device_id={"tm": peer, "chan": home}, device_id_type=MESH),
            pltpu.make_async_remote_copy(
                src_ref=scales.at[t], dst_ref=fscale_in.at[slot], send_sem=sidescale_send.at[(half + 1) * t + way],
                recv_sem=fscale_recv.at[slot], device_id={"tm": peer, "chan": home}, device_id_type=MESH),
        )

    def float_ways(t, started):
        def one(i, _):
            way = half - i

            @pl.when(jnp.logical_or(way > 0, core != home))
            def _():
                for copy in float_copies(t, way):
                    if started:
                        copy.wait_send()
                    else:
                        copy.start()
            return 0

        lax.fori_loop(0, half + 1, one, 0)

    back = SPAN - 1 - lax.broadcasted_iota(jnp.int32, (rows, SPAN), 1)

    def finish(t):
        sibling_copy(t).wait_recv()
        total = acc[t, core] + sib[t]
        total = jnp.take_along_axis(total, back, axis=1)
        top = jnp.maximum(jnp.max(jnp.abs(total), axis=0, keepdims=True), 1e-37)
        coded = jnp.round((total * (1.0 / top)) * CODES).astype(jnp.int32).astype(jnp.int16)
        scale = top * (1.0 / CODES)
        codes[t] = coded
        scales[t] = scale
        direct = t >= nf

        @pl.when(jnp.logical_and(direct, jnp.logical_not(jnp.logical_and(shard_of(t) == z, core == home))))
        def _():
            for copy in direct_copies(t, core):
                copy.start()

        @pl.when(jnp.logical_and(direct, jnp.logical_and(shard_of(t) == z, core == home)))
        def _():
            direct_in[own_part * 2 + core] = coded
            dscale_in[own_part * 2 + core] = scale

        @pl.when(jnp.logical_not(direct))
        def _():
            float_ways(t, False)

            @pl.when(core == home)
            def _():
                float_in[own_part * 2 * nf + 2 * t + core] = coded
                fscale_in[own_part * 2 * nf + 2 * t + core] = scale

    def float_arrival(slot):
        return (
            pltpu.make_async_remote_copy(
                src_ref=float_in.at[slot], dst_ref=float_in.at[slot], send_sem=fwd_send.at[slot],
                recv_sem=float_recv.at[slot], device_id=other, device_id_type=MESH),
            pltpu.make_async_remote_copy(
                src_ref=fscale_in.at[slot], dst_ref=fscale_in.at[slot], send_sem=fwdscale_send.at[slot],
                recv_sem=fscale_recv.at[slot], device_id=other, device_id_type=MESH),
        )

    def forward_copies(slot, step):
        to = {"tm": home * half + lax.rem(own_part + step, half), "chan": core}
        at = slot * half + step
        return (
            pltpu.make_async_remote_copy(
                src_ref=float_in.at[slot], dst_ref=float_in.at[slot], send_sem=fwd_send.at[at],
                recv_sem=float_recv.at[slot], device_id=to, device_id_type=MESH),
            pltpu.make_async_remote_copy(
                src_ref=fscale_in.at[slot], dst_ref=fscale_in.at[slot], send_sem=fwdscale_send.at[at],
                recv_sem=fscale_recv.at[slot], device_id=to, device_id_type=MESH),
        )

    def hand_on(started):
        @pl.when(jnp.logical_and(is_gate, core != home))
        def _():
            def one(slot, _):
                if not started:
                    for copy in float_arrival(slot):
                        copy.wait_recv()

                def on(step, _):
                    for copy in forward_copies(slot, step):
                        if started:
                            copy.wait_send()
                        else:
                            copy.start()
                    return 0

                lax.fori_loop(1, half, on, 0)
                return 0

            lax.fori_loop(0, half * 2 * nf, one, 0)

    energy_copy = pltpu.make_async_remote_copy(
        src_ref=e_mine, dst_ref=e_sib, send_sem=e_send, recv_sem=e_recv, device_id=other, device_id_type=MESH)

    def energies():
        for part in range(2):
            for b in range(slots):
                piece = rec_all[z + part, :, b * SPAN:(b + 1) * SPAN].astype(jnp.float32)
                e_mine[part * slots + b:part * slots + b + 1, :] = jnp.sum(piece * piece, axis=0, keepdims=True)
        energy_copy.start()

    def inverses():
        energy_copy.wait()
        e = e_mine[...] + e_sib[...]
        i0 = lax.broadcasted_iota(jnp.int32, (SPAN, SPAN), 0)
        i1 = lax.broadcasted_iota(jnp.int32, (SPAN, SPAN), 1)
        exact = functools.partial(jnp.dot, preferred_element_type=jnp.float32, precision=lax.Precision.HIGHEST)
        tails = exact(e, jnp.where(i0 >= i1, 1.0, 0.0))
        heads = exact(e, jnp.where(i0 < i1, 1.0, 0.0))
        sums = jnp.sum(e, axis=1, keepdims=True)
        for b in range(slots):
            energy = tails[b:b + 1] + heads[b + 4:b + 5] + sums[b + 1:b + 2] + sums[b + 2:b + 3] + sums[b + 3:b + 4]
            e_mine[b:b + 1, :] = lax.rsqrt(energy / (2 * chans * TAPS * SPAN) + 1e-05)

    build(0, 0)
    build(0, 1)

    def step(t, _):
        following = jnp.minimum(t + 1, chunks - 1)
        build(t, 2)
        product = dot(0)
        build(t, 3)
        product += dot(1)
        build(following, 0)
        product += dot(2)
        build(following, 1)
        product += dot(3)
        acc[t] = jnp.stack([product[:, :SPAN], product[:, SPAN:]])
        sibling_copy(t).start()

        @pl.when(t > 0)
        def _():
            finish(t - 1)

        return 0

    lax.fori_loop(0, chunks, step, 0)
    energies()
    finish(chunks - 1)
    hand_on(False)
    inverses()

    def put(part, slot, values, scale, inverse):
        out_ref[part * rows:(part + 1) * rows, slot * SPAN:(slot + 1) * SPAN] = values.astype(jnp.int32).astype(jnp.float32) * (scale * inverse)

    at = [span_all[z, 0, q] for q in range(slots)]
    inverse = [jnp.where(b >= 0, e_mine[pl.ds(jnp.maximum(b, 0), 1), :], 0.0) for b in at]
    for part in range(half):
        source = core * half + part
        for q in range(2):
            @pl.when(jnp.logical_not(jnp.logical_and(source == z, core == q)))
            def _():
                slot = part * 2 + q
                pltpu.make_async_remote_copy(
                    src_ref=codes.at[0], dst_ref=direct_in.at[slot], send_sem=code_send.at[0],
                    recv_sem=direct_recv.at[slot], device_id=other, device_id_type=MESH).wait_recv()
                pltpu.make_async_remote_copy(
                    src_ref=scales.at[0], dst_ref=dscale_in.at[slot], send_sem=scale_send.at[0],
                    recv_sem=dscale_recv.at[slot], device_id=other, device_id_type=MESH).wait_recv()

            put(part, q, direct_in[part * 2 + q], dscale_in[part * 2 + q], inverse[q])

    @pl.when(jnp.logical_not(jnp.logical_and(is_gate, core != home)))
    def _():
        def one(slot, _):
            part, f = slot // (2 * nf), lax.rem(slot, 2 * nf)

            @pl.when(jnp.logical_not(jnp.logical_and(core == home, jnp.logical_and(part == own_part, lax.rem(f, 2) == core))))
            def _():
                for copy in float_arrival(slot):
                    copy.wait_recv()
            return 0

        lax.fori_loop(0, half * 2 * nf, one, 0)

    def earlier(i, count):
        before = jnp.where(i // (slots - 2) < z, 1, 0)
        return count + before * jnp.where(span_all[i // (slots - 2), 0, 2 + i % (slots - 2)] >= 0, 1, 0)

    first = lax.fori_loop(0, n * (slots - 2), earlier, jnp.int32(0))
    for q in range(2, slots):
        f = jnp.minimum(first + q - 2, 2 * nf - 1)
        for part in range(half):
            put(part, q, float_in[part * 2 * nf + f], fscale_in[part * 2 * nf + f], inverse[q])

    def drain(t, _):
        sibling_copy(t).wait_send()

        @pl.when(jnp.logical_and(t >= nf, jnp.logical_not(jnp.logical_and(shard_of(t) == z, core == home))))
        def _():
            for copy in direct_copies(t, core):
                copy.wait_send()

        @pl.when(t < nf)
        def _():
            float_ways(t, True)

        return 0

    lax.fori_loop(0, chunks, drain, 0)
    hand_on(True)

    def sent(i, _):
        for copy in record_copies(i, True):
            copy.wait_send()
        return 0

    lax.fori_loop(1, n, sent, 0)


def local(n, record, templates, span_list):
    _, rows, chans, _ = templates.shape
    slots = span_list.shape[1]
    nf = float_chunks(n)
    chunks = nf + n
    half = n // 2
    hbm = pl.BlockSpec(memory_space=pltpu.HBM)
    dma = pltpu.SemaphoreType.DMA
    hank = pltpu.VMEM((chans, SPAN, 2 * SPAN), jnp.bfloat16)
    return pl.pallas_call(
        functools.partial(kernel, n, rows, chans, slots),
        out_shape=pltpu.VMEM((rows * half, slots * SPAN), jnp.float32),
        in_specs=[hbm, hbm, hbm],
        out_specs=pl.BlockSpec(memory_space=pltpu.VMEM),
        scratch_shapes=[
            pltpu.VMEM(templates.shape[1:], jnp.bfloat16),
            pltpu.VMEM((TAPS * rows, chans * SPAN), jnp.bfloat16),
            pltpu.VMEM((n + 1, chans, record.shape[1]), jnp.bfloat16),
            pltpu.SMEM((n, 1, slots), jnp.int32),
            pltpu.SMEM((chunks, 2), jnp.int32),
            pltpu.VMEM((n * slots + TAPS + 1, chans, 16, SPAN), jnp.bfloat16),
            hank, hank, hank, hank,
            pltpu.VMEM((chunks, 2, rows, SPAN), jnp.float32),
            pltpu.VMEM((chunks, rows, SPAN), jnp.float32),
            pltpu.VMEM((chunks, rows, SPAN), jnp.int16),
            pltpu.VMEM((chunks, 1, SPAN), jnp.float32),
            pltpu.VMEM((half * 2, rows, SPAN), jnp.int16),
            pltpu.VMEM((half * 2, 1, SPAN), jnp.float32),
            pltpu.VMEM((half * 2 * nf, rows, SPAN), jnp.int16),
            pltpu.VMEM((half * 2 * nf, 1, SPAN), jnp.float32),
            pltpu.VMEM((8, SPAN), jnp.float32),
            pltpu.VMEM((8, SPAN), jnp.float32),
            dma, dma, dma((3,)), dma((n,)), dma((n,)), dma((n,)), dma((n,)),
            dma((chunks,)), dma((chunks,)), dma((chunks,)), dma((chunks,)), dma(((half + 1) * nf,)), dma(((half + 1) * nf,)),
            dma((half * 2,)), dma((half * 2,)), dma((half * 2 * nf,)), dma((half * 2 * nf,)),
            dma((half * half * 2 * nf,)), dma((half * half * 2 * nf,)), dma, dma,
        ],
        compiler_params=pltpu.CompilerParams(collective_id=0, has_side_effects=True, vmem_limit_bytes=40 * 2**20),
    )(*(pltpu.with_memory_space_constraint(x, pltpu.HBM) for x in (span_list, record, templates)))


def solution(mesh):
    in_specs = (P("chan", ("grp", "tm")), P("tmpl", "tm", "chan", None), P(("grp", "tm"), None))
    out_specs = P(("tmpl", "chan"), ("grp", "tm"))
    return jax.shard_map(functools.partial(local, mesh.shape["tm"]), mesh=mesh, in_specs=in_specs, out_specs=out_specs, check_vma=False)
```
